32 devices in a mesh: dp: 32 (over z, y, x, core).
Axes of the slice: x: 2, y: 2, z: 4, core: 2. Of those that a mesh axis runs over, the one named last changes fastest.
Arguments:
- images: bfloat16 [64, 197, 384], P('dp'), may hold values from -6 to 6
- params: bfloat16 [1777664], P('dp'), may hold values from -1.2 to 1.4
- cotangent: bfloat16 [64, 197, 384], P('dp'), may hold values from -6 to 6
- counts: int32 [32], P('dp'), may hold values from 1 to 2, as said below
Outputs:
- block_out: bfloat16 [64, 197, 384], P('dp')
- image_grad: bfloat16 [64, 197, 384], P('dp')
- param_grad: float32 [1777664], P('dp')
The draws below stay inside these ranges and needn't reach their ends.
Inputs may be any that keep to these rules, and one draw needn't show every extreme that they name: `counts`: every device has 1 to 2 live images; some device has exactly 2 and some exactly 1.
All inputs are finite; a program needn't handle non-finite values.
Results may differ from the reference program's by a relative error of at most 0.0075.
Values may be sent and summed in bfloat16 or wider, within the bound.
No kernel may reach another device: no remote copies, remote signals or barrier semaphores. Data moves between devices by JAX's collectives and lax.ppermute only.
A program may use at most 128 MiB of HBM per device.

```python
import jax
import jax.numpy as jnp
from jax import lax

D = 384
HEADS = 6
FF = 1536
TOK = 197
IMG_DEV = 2
IMAGES = 64
NPARAM = 1774080
PARAMS = 1777664
N_DP = 32


def draw_params(key, part):
    table = [(3 * D * D, D ** (-0.5)), (D, 0.3), (D, 0.3), (D * D, 2.0 * D ** (-0.5)), (D, 0.3), (D * FF, D ** (-0.5)), (FF, 0.3), (FF * D, FF ** (-0.5)), (D, 0.3), (D, -1.0), (D, 0.3), (D, -1.0), (D, 0.3), (PARAMS - NPARAM, 0.3)]
    pieces = []
    for position, (entry_size, spread) in enumerate(table):
        sub_key = jax.random.fold_in(key, position + 11)
        sample = jnp.clip(jax.random.normal(sub_key, (entry_size,), jnp.float32), -4.0, 4.0)
        if spread < 0:
            pieces.append(1.0 + 0.1 * sample)
        else:
            pieces.append(spread * sample)
    return jnp.concatenate(pieces).astype(jnp.bfloat16)


def draw_counts(key, part):
    base_counts = jax.random.randint(jax.random.fold_in(key, 3), (N_DP,), 1, IMG_DEV + 1)
    high_spot = jax.random.randint(jax.random.fold_in(key, 5), (), 0, N_DP)
    low_spot = (high_spot + 1 + jax.random.randint(jax.random.fold_in(key, 7), (), 0, N_DP - 1)) % N_DP
    return base_counts.at[high_spot].set(IMG_DEV).at[low_spot].set(1).astype(jnp.int32)


def block_levels(key, dims, shards, low, high):
    gain, own = 1.0, jax.random.fold_in(key, 6)
    for dim, parts in shards:
        steps = jnp.exp(jax.random.uniform(jax.random.fold_in(own, dim), (parts,), jnp.float32, low / len(shards), high / len(shards)))
        gain = gain * jnp.repeat(steps, dims[dim] // parts).reshape([-1 if axis == dim else 1 for axis in range(len(dims))])
    return gain


def scatter_about(rng, extent, scale, bound, cuts=(), kind=jnp.bfloat16):
    values = jax.random.normal(rng, extent, jnp.float32) * scale
    if len(cuts) > 0:
        values = block_levels(rng, extent, cuts, -0.22, 0.18) * values
    return jnp.clip(values, min=-bound, max=bound).astype(kind)


def setup_inputs(seed: int = 0) -> dict:
    arg_keys = jax.random.split(jax.random.key(seed), 5)
    return {
        "images": scatter_about(arg_keys[0], (IMAGES, TOK, D), 1.0, 6.0, ((0, 32),)),
        "params": draw_params(jax.random.fold_in(arg_keys[4], 71), 0),
        "cotangent": scatter_about(arg_keys[2], (IMAGES, TOK, D), 1.0, 6.0, ((0, 32),)),
        "counts": draw_counts(jax.random.fold_in(arg_keys[4], 71), 0),
    }


@jax.custom_vjp
def low(v):
    return lax.optimization_barrier(v.astype(jnp.bfloat16)).astype(jnp.float32)

@jax.custom_vjp
def low_back(v):
    return v

def low_keep(v):
    return (low(v), None)

def low_pass(kept, grad):
    return (grad,)

def back_keep(v):
    return (v, None)

def back_low(kept, grad):
    return (low(grad),)
low.defvjp(low_keep, low_pass)
low_back.defvjp(back_keep, back_low)
EPSILON = 1e-06
HIGHEST = lax.Precision.HIGHEST

def param_layout():
    return [('w_qkv', (D, 3 * D)), ('b_query', (D,)), ('b_value', (D,)), ('w_out', (D, D)), ('b_out', (D,)), ('w_up', (D, FF)), ('b_up', (FF,)), ('w_down', (FF, D)), ('b_down', (D,)), ('g_first', (D,)), ('b_first', (D,)), ('g_second', (D,)), ('b_second', (D,))]

def unpack_flat(flat_buffer):
    pieces = {}
    position = 0
    for entry_name, entry_shape in param_layout():
        entry_size = 1
        for extent_value in entry_shape:
            entry_size = entry_size * extent_value
        pieces[entry_name] = flat_buffer[position:position + entry_size].reshape(entry_shape)
        position = position + entry_size
    return pieces

def standardize(values):
    centre = values - lax.optimization_barrier(jnp.mean(values, -1, keepdims=True))
    return centre * lax.rsqrt(lax.optimization_barrier(jnp.mean(centre * centre, -1, keepdims=True)) + EPSILON)

def round_both(values):
    return low_back(low(values))

def forward_pass(flat_buffer, image_block):
    weights = unpack_flat(flat_buffer)
    image_count = image_block.shape[0]
    head_size = D // HEADS
    tokens_in = image_block.reshape(-1, D)
    normed = low(standardize(tokens_in) * weights['g_first'] + weights['b_first'])
    joined = jnp.dot(normed, weights['w_qkv'], precision=HIGHEST)
    query = round_both(joined[:, :D] + weights['b_query']).reshape(image_count, TOK, HEADS, head_size)
    keys_all = round_both(joined[:, D:2 * D]).reshape(image_count, TOK, HEADS, head_size)
    values_all = round_both(joined[:, 2 * D:] + weights['b_value']).reshape(image_count, TOK, HEADS, head_size)
    scores = low_back(jnp.einsum('bqhd,bkhd->bhqk', query, keys_all, precision=HIGHEST) * float(head_size) ** (-0.5))
    probs = low(jax.nn.softmax(scores, axis=-1))
    mixed = round_both(jnp.einsum('bhqk,bkhd->bqhd', probs, values_all, precision=HIGHEST)).reshape(-1, D)
    attended = low_back(jnp.dot(mixed, weights['w_out'], precision=HIGHEST) + weights['b_out'])
    middle = tokens_in + attended
    second = low(standardize(middle) * weights['g_second'] + weights['b_second'])
    hidden_pre = low_back(jnp.dot(second, weights['w_up'], precision=HIGHEST) + weights['b_up'])
    hidden = low(jax.nn.gelu(hidden_pre, approximate=False))
    branch = low_back(jnp.dot(hidden, weights['w_down'], precision=HIGHEST) + weights['b_down'])
    return (middle + branch).reshape(image_block.shape)

def reference(images, params, cotangent, counts):
    flat_buffer = params.astype(jnp.float32)
    slot_index = jnp.arange(IMAGES, dtype=jnp.int32)
    live = (slot_index % IMG_DEV < counts[slot_index // IMG_DEV]).astype(jnp.float32)
    inputs_all = images.astype(jnp.float32).reshape(N_DP, IMG_DEV, TOK, D)
    grads_all = (cotangent.astype(jnp.float32) * live[:, None, None]).reshape(N_DP, IMG_DEV, TOK, D)

    def group_step(total, item):
        image_block, grad_block = item
        result, pull_back = jax.vjp(forward_pass, flat_buffer, image_block)
        grad_flat, grad_images = pull_back(grad_block)
        return (total + grad_flat, (result.astype(jnp.bfloat16), grad_images.astype(jnp.bfloat16)))
    total, (results, grad_images) = lax.scan(group_step, jnp.zeros((PARAMS,), jnp.float32), (inputs_all, grads_all))
    return (results.reshape(IMAGES, TOK, D), grad_images.reshape(IMAGES, TOK, D), total)
```

```python
import jax
import jax.numpy as jnp
from jax import lax
from jax.experimental import pallas as pl
from jax.experimental.pallas import tpu as pltpu
from jax.sharding import PartitionSpec as P

D = 384
HEADS = 6
FF = 1536
LANES = 128
EPSILON = 1e-06
SQRT_HALF = 0.7071067811865476
INV_ROOT_TAU = 0.3989422804014327
BF = jnp.bfloat16
F32 = jnp.float32

R_QKV = 0
R_BQ = R_QKV + D * 3 * D // LANES
R_BV = R_BQ + D // LANES
R_OUT = R_BV + D // LANES
R_BO = R_OUT + D * D // LANES
R_UP = R_BO + D // LANES
R_BU = R_UP + D * FF // LANES
R_DOWN = R_BU + FF // LANES
R_BD = R_DOWN + D * FF // LANES
R_G1 = R_BD + D // LANES
R_B1 = R_G1 + D // LANES
R_G2 = R_B1 + D // LANES
R_B2 = R_G2 + D // LANES
R_END = R_B2 + D // LANES


def dot_nn(a, b):
    return lax.dot_general(a, b, (((1,), (0,)), ((), ())), preferred_element_type=F32)


def dot_nt(a, b):
    return lax.dot_general(a, b, (((1,), (1,)), ((), ())), preferred_element_type=F32)


def dot_tn(a, b):
    return lax.dot_general(a, b, (((0,), (0,)), ((), ())), preferred_element_type=F32)


def row_vector(ref, row, count):
    return jnp.concatenate([ref[row + i : row + i + 1, :] for i in range(count)], axis=1)


def put_row_vector(ref, row, value):
    for i in range(value.shape[1] // LANES):
        ref[row + i : row + i + 1, :] = value[:, i * LANES : (i + 1) * LANES]


def fold_rows(value):
    return jnp.sum(value.reshape(-1, 8, value.shape[-1]), axis=0)


def layer_body(
    me_ref,
    count_ref,
    image_ref,
    cot_ref,
    *refs,
    devices,
    rows,
    images,
    tok,
    pad,
):
    pieces = refs[:devices]
    (out_ref, gin_ref, send_ref, keep_ref) = refs[devices : devices + 4]
    (
        stage,
        wide,
        wq,
        wo,
        wu,
        wd,
        x_s,
        n1_s,
        r1_s,
        normed,
        qkv,
        probs,
        mixed,
        mid_s,
        n2_s,
        r2_s,
        second,
        hidden,
        gpre,
        acc,
        acc2,
        glow,
        gattn,
        gmix,
        gj,
        sems,
    ) = refs[devices + 4 :]
    me = me_ref[0]
    total = images * pad
    scale = float(D // HEADS) ** (-0.5)
    blk = 32
    steps = total // blk
    copies = [
        pltpu.make_async_copy(pieces[k], stage.at[me ^ k], sems.at[k]) for k in range(devices)
    ]
    for c in copies:
        c.start()

    for b in range(images):
        live = (count_ref[0] > b).astype(F32)
        zeros = jnp.zeros((pad - tok, D), F32)
        x_s[b * pad : (b + 1) * pad, :] = jnp.concatenate(
            [image_ref[b].astype(F32), zeros], axis=0
        )
        glow[b * pad : (b + 1) * pad, :] = jnp.concatenate(
            [cot_ref[b].astype(F32) * live, zeros], axis=0
        ).astype(BF)

    for c in copies:
        c.wait()
    for d in range(devices):
        wide[d * rows : (d + 1) * rows, :] = stage[d].astype(F32)

    def unpack(dst, start, height, width):
        per = width // LANES
        for j in range(per):
            dst[:, j * LANES : (j + 1) * LANES] = wide[
                pl.ds(start + j, height, stride=per), :
            ].astype(BF)

    unpack(wq, R_QKV, D, 3 * D)
    unpack(wo, R_OUT, D, D)
    unpack(wu, R_UP, D, FF)
    unpack(wd, R_DOWN, FF, D)
    b_query = row_vector(wide, R_BQ, 3)
    b_value = row_vector(wide, R_BV, 3)
    b_out = row_vector(wide, R_BO, 3)
    b_up = row_vector(wide, R_BU, 12)
    b_down = row_vector(wide, R_BD, 3)
    g_first = row_vector(wide, R_G1, 3)
    b_first = row_vector(wide, R_B1, 3)
    g_second = row_vector(wide, R_G2, 3)
    b_second = row_vector(wide, R_B2, 3)

    def blocks(body, init=None):
        def step(i, carry):
            return body(pl.ds(pl.multiple_of(i * blk, blk), blk), carry)

        return lax.fori_loop(0, steps, step, init)

    def standardize(v):
        centre = v - jnp.mean(v, axis=-1, keepdims=True)
        inverse = lax.rsqrt(jnp.mean(centre * centre, axis=-1, keepdims=True) + EPSILON)
        return centre * inverse, inverse

    def first_norm(at, carry):
        hat, inverse = standardize(x_s[at, :])
        n1_s[at, :] = hat
        r1_s[at, :] = inverse
        normed[at, :] = (hat * g_first + b_first).astype(BF)
        return carry

    blocks(first_norm)

    qkv[:, :D] = (dot_nn(normed[...], wq[:, :D]) + b_query).astype(BF)
    qkv[:, D : 2 * D] = dot_nn(normed[...], wq[:, D : 2 * D]).astype(BF)
    qkv[:, 2 * D :] = (dot_nn(normed[...], wq[:, 2 * D :]) + b_value).astype(BF)

    lane = lax.broadcasted_iota(jnp.int32, (1, LANES), 1)
    low_lane = lane < D // HEADS
    halves = (low_lane.astype(F32).astype(BF), (1.0 - low_lane.astype(F32)).astype(BF))
    key_ok = lax.broadcasted_iota(jnp.int32, (1, pad), 1) < tok

    def slab(ref, b, column):
        return ref[b * pad : (b + 1) * pad, column : column + LANES]

    for b in range(images):
        for h in range(HEADS // 2):
            query = slab(qkv, b, h * LANES)
            keys = slab(qkv, b, D + h * LANES)
            values = slab(qkv, b, 2 * D + h * LANES)
            outs = []
            for s in range(2):
                scores = jnp.where(key_ok, dot_nt(query * halves[s], keys) * scale, -1e30)
                top = jnp.max(scores, axis=-1, keepdims=True)
                weight = jnp.exp(scores - top)
                prob = weight * (1.0 / jnp.sum(weight, axis=-1, keepdims=True))
                probs[(b * HEADS // 2 + h) * 2 + s] = prob
                outs.append(dot_nn(prob.astype(BF), values))
            mixed[b * pad : (b + 1) * pad, h * LANES : (h + 1) * LANES] = jnp.where(
                low_lane, outs[0], outs[1]
            ).astype(BF)

    acc[...] = dot_nn(mixed[...], wo[...])

    def second_norm(at, carry):
        middle = x_s[at, :] + (acc[at, :] + b_out)
        mid_s[at, :] = middle
        hat, inverse = standardize(middle)
        n2_s[at, :] = hat
        r2_s[at, :] = inverse
        second[at, :] = (hat * g_second + b_second).astype(BF)
        return carry

    blocks(second_norm)

    wide[R_END:, :] = jnp.zeros((devices * rows - R_END, LANES), F32)

    def scatter(value, start, per):
        for j in range(value.shape[1] // LANES):
            wide[pl.ds(start + j, value.shape[0], stride=per), :] = value[
                :, j * LANES : (j + 1) * LANES
            ]

    for c in range(FF // D):
        cols = slice(c * D, (c + 1) * D)
        acc[...] = dot_nn(second[...], wu[:, cols])
        acc2[...] = dot_nt(glow[...], wd[cols, :])
        bias = b_up[:, cols]

        def activate(at, carry, cols=cols, bias=bias):
            pre = acc[at, :] + bias
            cdf = 0.5 * (1.0 + lax.erf(pre * SQRT_HALF))
            hidden[at, cols] = (pre * cdf).astype(BF)
            slope = cdf + pre * INV_ROOT_TAU * jnp.exp(-0.5 * pre * pre)
            back = (acc2[at, :] * slope).astype(BF)
            gpre[at, cols] = back
            return carry + fold_rows(back.astype(F32))

        sums = blocks(activate, jnp.zeros((8, D), F32))
        put_row_vector(wide, R_BU + 3 * c, jnp.sum(sums, axis=0, keepdims=True))
        scatter(dot_tn(second[...], gpre[:, cols]), R_UP + 3 * c, FF // LANES)
        scatter(dot_tn(hidden[:, cols], glow[...]), R_DOWN + 3 * D * c, D // LANES)

    acc[...] = dot_nn(hidden[...], wd[...])
    acc2[...] = dot_nt(gpre[...], wu[...])

    def second_back(at, carry):
        sum_g, sum_b, sum_low, sum_attn = carry
        grad = acc2[at, :]
        hat = n2_s[at, :]
        low = glow[at, :].astype(F32)
        mixed_block = mid_s[at, :] + (acc[at, :] + b_down)
        gmix[at, :] = mixed_block.astype(BF)
        s = grad * g_second
        middle_grad = low + r2_s[at, :] * (
            s
            - jnp.mean(s, axis=-1, keepdims=True)
            - hat * jnp.mean(s * hat, axis=-1, keepdims=True)
        )
        mid_s[at, :] = middle_grad
        attn = middle_grad.astype(BF)
        gattn[at, :] = attn
        return (
            sum_g + fold_rows(grad * hat),
            sum_b + fold_rows(grad),
            sum_low + fold_rows(low),
            sum_attn + fold_rows(attn.astype(F32)),
        )

    zero8 = jnp.zeros((8, D), F32)
    sum_g, sum_b, sum_low, sum_attn = blocks(second_back, (zero8, zero8, zero8, zero8))

    def put_sum(row, value):
        put_row_vector(wide, row, jnp.sum(value, axis=0, keepdims=True))

    put_sum(R_G2, sum_g)
    put_sum(R_B2, sum_b)
    put_sum(R_BD, sum_low)
    put_sum(R_BO, sum_attn)
    for b in range(images):
        out_ref[b] = gmix[b * pad : b * pad + tok, :]

    scatter(dot_tn(mixed[...], gattn[...]), R_OUT, D // LANES)
    gmix[...] = dot_nt(gattn[...], wo[...]).astype(BF)

    for b in range(images):
        for h in range(HEADS // 2):
            query = slab(qkv, b, h * LANES)
            keys = slab(qkv, b, D + h * LANES)
            values = slab(qkv, b, 2 * D + h * LANES)
            grads = slab(gmix, b, h * LANES)
            parts = []
            for s in range(2):
                prob = probs[(b * HEADS // 2 + h) * 2 + s]
                grad_prob = dot_nt(grads * halves[s], values)
                total_s = jnp.sum(grad_prob * prob, axis=-1, keepdims=True)
                grad_score = (prob * (grad_prob - total_s)).astype(BF)
                parts.append(
                    (
                        dot_nn(grad_score, keys) * scale,
                        dot_tn(grad_score, query) * scale,
                        dot_tn(prob.astype(BF), grads),
                    )
                )
            for t in range(3):
                column = t * D + h * LANES
                gj[b * pad : (b + 1) * pad, column : column + LANES] = jnp.where(
                    low_lane, parts[0][t], parts[1][t]
                ).astype(BF)

    for t in range(3):
        scatter(dot_tn(normed[...], gj[:, t * D : (t + 1) * D]), R_QKV + 3 * t, 3 * D // LANES)
    acc[...] = dot_nt(gj[...], wq[...])

    def first_back(at, carry):
        sum_g, sum_b, sum_q, sum_v = carry
        grad = acc[at, :]
        hat = n1_s[at, :]
        s = grad * g_first
        result = mid_s[at, :] + r1_s[at, :] * (
            s
            - jnp.mean(s, axis=-1, keepdims=True)
            - hat * jnp.mean(s * hat, axis=-1, keepdims=True)
        )
        gmix[at, :] = result.astype(BF)
        return (
            sum_g + fold_rows(grad * hat),
            sum_b + fold_rows(grad),
            sum_q + fold_rows(gj[at, :D].astype(F32)),
            sum_v + fold_rows(gj[at, 2 * D :].astype(F32)),
        )

    sum_g, sum_b, sum_q, sum_v = blocks(first_back, (zero8, zero8, zero8, zero8))
    put_sum(R_G1, sum_g)
    put_sum(R_B1, sum_b)
    put_sum(R_BQ, sum_q)
    put_sum(R_BV, sum_v)
    for b in range(images):
        gin_ref[b] = gmix[b * pad : b * pad + tok, :]

    for d in range(devices):
        stage[d] = wide[d * rows : (d + 1) * rows, :].astype(BF)
    copies = []
    for k in range(devices):
        target = (send_ref if k & 1 else keep_ref).at[k >> 1]
        copies.append(pltpu.make_async_copy(stage.at[me ^ k], target, sems.at[k]))
    for c in copies:
        c.start()
    for c in copies:
        c.wait()


def run_layer(me, counts, images, cotangent, pieces, interpret=False):
    devices = len(pieces)
    rows = pieces[0].shape[0]
    count, tok, _ = images.shape
    pad = (tok + 15) // 16 * 16
    total = count * pad
    body = lambda *refs: layer_body(
        *refs, devices=devices, rows=rows, images=count, tok=tok, pad=pad
    )
    vmem = pl.BlockSpec(memory_space=pltpu.VMEM)
    smem = pl.BlockSpec(memory_space=pltpu.SMEM)
    anyspace = pl.BlockSpec(memory_space=pl.ANY)
    half = jax.ShapeDtypeStruct((devices // 2, rows, LANES), BF)
    act = jax.ShapeDtypeStruct(images.shape, BF)
    V = pltpu.VMEM
    scratch = [
        V((devices, rows, LANES), BF),
        V((devices * rows, LANES), F32),
        V((D, 3 * D), BF),
        V((D, D), BF),
        V((D, FF), BF),
        V((FF, D), BF),
        V((total, D), F32),
        V((total, D), F32),
        V((total, 1), F32),
        V((total, D), BF),
        V((total, 3 * D), BF),
        V((count * HEADS, pad, pad), F32),
        V((total, D), BF),
        V((total, D), F32),
        V((total, D), F32),
        V((total, 1), F32),
        V((total, D), BF),
        V((total, FF), BF),
        V((total, FF), BF),
        V((total, D), F32),
        V((total, D), F32),
        V((total, D), BF),
        V((total, D), BF),
        V((total, D), BF),
        V((total, 3 * D), BF),
        pltpu.SemaphoreType.DMA((devices,)),
    ]
    return pl.pallas_call(
        body,
        name="layer",
        out_shape=(act, act, half, half),
        in_specs=[smem, smem, vmem, vmem] + [anyspace] * devices,
        out_specs=(vmem, vmem, anyspace, anyspace),
        scratch_shapes=scratch,
        compiler_params=pltpu.CompilerParams(vmem_limit_bytes=48 << 20),
        interpret=interpret,
    )(me, counts, images, cotangent, *pieces)


def swap(value, mask, devices):
    return lax.ppermute(value, "dp", [(i, i ^ mask) for i in range(devices)])


def gather_pieces(own, devices):
    pieces = {0: own}
    for s in range(8, devices, 8):
        pieces[s] = swap(own, s, devices)
    outer = sorted(pieces)
    for s in outer:
        pieces[s | 2] = swap(pieces[s], 2, devices)
        pieces[s | 4] = swap(pieces[s], 4, devices)
    for i, s in enumerate(outer):
        if i % 2 == 0:
            pieces[s | 6] = swap(pieces[s | 2], 4, devices)
        else:
            pieces[s | 6] = swap(pieces[s | 4], 2, devices)
    for s in sorted(pieces):
        pieces[s | 1] = swap(pieces[s], 1, devices)
    return [pieces[k] for k in range(devices)]


def reduce_pieces(keep, send, devices):
    held = keep.astype(F32) + swap(send, 1, devices).astype(F32)
    outer = devices // 8
    rows = keep.shape[1]
    held = held.reshape(outer, 2, 2, rows, LANES).astype(BF)
    cut = outer // 2
    up, down = held[:cut], held[cut:]
    up_got = swap(up[:, :, 1], 2, devices)
    down_got = swap(down[:, 1], 4, devices)
    up = (up[:, :, 0].astype(F32) + up_got.astype(F32)).astype(BF)
    down = (down[:, 0].astype(F32) + down_got.astype(F32)).astype(BF)
    up_got = swap(up[:, 1], 4, devices)
    down_got = swap(down[:, 1], 2, devices)
    up = up[:, 0].astype(F32) + up_got.astype(F32)
    down = down[:, 0].astype(F32) + down_got.astype(F32)
    mine = [up[i] for i in range(cut)] + [down[i] for i in range(outer - cut)]
    total = mine[0]
    for s in range(1, outer):
        total = total + swap(mine[s].astype(BF), 8 * s, devices).astype(F32)
    return total


def on_device(images, params, cotangent, counts):
    devices = lax.axis_size("dp")
    own = params.reshape(-1, LANES)
    pieces = gather_pieces(own, devices)
    me = lax.axis_index("dp").astype(jnp.int32).reshape(1)
    result, image_grad, send, keep = run_layer(me, counts, images, cotangent, pieces)
    owned = reduce_pieces(keep, send, devices)
    return (result, image_grad, owned.reshape(-1))


def solution(mesh):
    placed = (P("dp", None, None), P("dp"), P("dp", None, None), P("dp"))
    return jax.shard_map(
        on_device,
        mesh=mesh,
        in_specs=placed,
        out_specs=(P("dp", None, None), P("dp", None, None), P("dp")),
        check_vma=False,
    )
```

```python
import jax
import jax.numpy as jnp
from jax import lax
from jax.experimental import pallas as pl
from jax.experimental.pallas import tpu as pltpu
from jax.sharding import PartitionSpec as P

D = 384
HEADS = 6
FF = 1536
LANES = 128
EPSILON = 1e-06
SQRT_HALF = 0.7071067811865476
INV_ROOT_TAU = 0.3989422804014327
BF = jnp.bfloat16
F32 = jnp.float32

R_QKV = 0
R_BQ = R_QKV + D * 3 * D // LANES
R_BV = R_BQ + D // LANES
R_OUT = R_BV + D // LANES
R_BO = R_OUT + D * D // LANES
R_UP = R_BO + D // LANES
R_BU = R_UP + D * FF // LANES
R_DOWN = R_BU + FF // LANES
R_BD = R_DOWN + D * FF // LANES
R_G1 = R_BD + D // LANES
R_B1 = R_G1 + D // LANES
R_G2 = R_B1 + D // LANES
R_B2 = R_G2 + D // LANES
R_END = R_B2 + D // LANES


def dot_nn(a, b):
    return lax.dot_general(a, b, (((1,), (0,)), ((), ())), preferred_element_type=F32)


def dot_nt(a, b):
    return lax.dot_general(a, b, (((1,), (1,)), ((), ())), preferred_element_type=F32)


def dot_tn(a, b):
    return lax.dot_general(a, b, (((0,), (0,)), ((), ())), preferred_element_type=F32)


def row_vector(ref, row, count):
    return jnp.concatenate([ref[row + i : row + i + 1, :] for i in range(count)], axis=1)


def put_row_vector(ref, row, value):
    for i in range(value.shape[1] // LANES):
        ref[row + i : row + i + 1, :] = value[:, i * LANES : (i + 1) * LANES]


def fold_rows(value):
    return jnp.sum(value.reshape(-1, 8, value.shape[-1]), axis=0)


def low_bits(me, c, b2, b1):
    first = 2 + 2 * ((me & 1) ^ c)
    return (me & 7) ^ c ^ (b1 * first) ^ (b2 * (6 - first))


def group_keys(devices):
    outer = devices // 8
    near, far = tuple(range(outer // 2)), tuple(range(outer // 2, outer))
    return [(c, b2, shifts) for shifts in (near, far) for c in range(2) for b2 in range(2)]


def layer_body(
    me_ref,
    count_ref,
    image_ref,
    cot_ref,
    *refs,
    devices,
    rows,
    images,
    tok,
    pad,
):
    order = group_keys(devices)
    groups = refs[: len(order)]
    refs = refs[len(order) :]
    out_ref, gin_ref = refs[:2]
    shares = refs[2 : 2 + len(order)]
    (
        stage,
        wide,
        wq,
        wo,
        wu,
        wd,
        x_s,
        n1_s,
        r1_s,
        normed,
        qkv,
        probs,
        mixed,
        mid_s,
        n2_s,
        r2_s,
        second,
        hidden,
        gpre,
        acc,
        acc2,
        glow,
        gattn,
        gmix,
        gj,
        sems,
    ) = refs[2 + len(order) :]
    me = me_ref[0]
    total = images * pad
    scale = float(D // HEADS) ** (-0.5)
    blk = 32
    steps = total // blk
    plane = me >> 3

    def slots(refs):
        for ref, (c, b2, shifts) in zip(refs, order):
            for i in range(2 * len(shifts)):
                b1, s = divmod(i, len(shifts))
                yield ref.at[i], ((plane ^ shifts[s]) << 3) | low_bits(me, c, b2, b1)

    for b in range(images):
        live = (count_ref[0] > b).astype(F32)
        zeros = jnp.zeros((pad - tok, D), F32)
        x_s[b * pad : (b + 1) * pad, :] = jnp.concatenate(
            [image_ref[b].astype(F32), zeros], axis=0
        )
        glow[b * pad : (b + 1) * pad, :] = jnp.concatenate(
            [cot_ref[b].astype(F32) * live, zeros], axis=0
        ).astype(BF)

    for ref, owner in slots(groups):
        wide[pl.ds(owner * rows, rows), :] = ref[...].astype(F32)

    def unpack(dst, start, height, width):
        per = width // LANES
        for j in range(per):
            dst[:, j * LANES : (j + 1) * LANES] = wide[
                pl.ds(start + j, height, stride=per), :
            ].astype(BF)

    unpack(wq, R_QKV, D, 3 * D)
    unpack(wo, R_OUT, D, D)
    unpack(wu, R_UP, D, FF)
    unpack(wd, R_DOWN, FF, D)
    b_query = row_vector(wide, R_BQ, 3)
    b_value = row_vector(wide, R_BV, 3)
    b_out = row_vector(wide, R_BO, 3)
    b_up = row_vector(wide, R_BU, 12)
    b_down = row_vector(wide, R_BD, 3)
    g_first = row_vector(wide, R_G1, 3)
    b_first = row_vector(wide, R_B1, 3)
    g_second = row_vector(wide, R_G2, 3)
    b_second = row_vector(wide, R_B2, 3)

    def blocks(body, init=None):
        def step(i, carry):
            return body(pl.ds(pl.multiple_of(i * blk, blk), blk), carry)

        return lax.fori_loop(0, steps, step, init, unroll=True)

    def standardize(v):
        centre = v - jnp.mean(v, axis=-1, keepdims=True)
        inverse = lax.rsqrt(jnp.mean(centre * centre, axis=-1, keepdims=True) + EPSILON)
        return centre * inverse, inverse

    def first_norm(at, carry):
        hat, inverse = standardize(x_s[at, :])
        n1_s[at, :] = hat
        r1_s[at, :] = inverse
        normed[at, :] = (hat * g_first + b_first).astype(BF)
        return carry

    blocks(first_norm)

    qkv[:, :D] = (dot_nn(normed[...], wq[:, :D]) + b_query).astype(BF)
    qkv[:, D : 2 * D] = dot_nn(normed[...], wq[:, D : 2 * D]).astype(BF)
    qkv[:, 2 * D :] = (dot_nn(normed[...], wq[:, 2 * D :]) + b_value).astype(BF)

    lane = lax.broadcasted_iota(jnp.int32, (1, LANES), 1)
    low_lane = lane < D // HEADS
    halves = (low_lane.astype(F32).astype(BF), (1.0 - low_lane.astype(F32)).astype(BF))
    key_ok = lax.broadcasted_iota(jnp.int32, (1, pad), 1) < tok

    def slab(ref, b, column):
        return ref[b * pad : (b + 1) * pad, column : column + LANES]

    for b in range(images):
        for h in range(HEADS // 2):
            query = slab(qkv, b, h * LANES)
            keys = slab(qkv, b, D + h * LANES)
            values = slab(qkv, b, 2 * D + h * LANES)
            outs = []
            for s in range(2):
                scores = jnp.where(key_ok, dot_nt(query * halves[s], keys) * scale, -1e30)
                top = jnp.max(scores, axis=-1, keepdims=True)
                weight = jnp.exp(scores - top)
                prob = weight * (1.0 / jnp.sum(weight, axis=-1, keepdims=True))
                probs[(b * HEADS // 2 + h) * 2 + s] = prob
                outs.append(dot_nn(prob.astype(BF), values))
            mixed[b * pad : (b + 1) * pad, h * LANES : (h + 1) * LANES] = jnp.where(
                low_lane, outs[0], outs[1]
            ).astype(BF)

    acc[...] = dot_nn(mixed[...], wo[...])

    def second_norm(at, carry):
        middle = x_s[at, :] + (acc[at, :] + b_out)
        mid_s[at, :] = middle
        hat, inverse = standardize(middle)
        n2_s[at, :] = hat
        r2_s[at, :] = inverse
        second[at, :] = (hat * g_second + b_second).astype(BF)
        return carry

    blocks(second_norm)

    wide[R_END:, :] = jnp.zeros((devices * rows - R_END, LANES), F32)

    def scatter(value, start, per):
        for j in range(value.shape[1] // LANES):
            wide[pl.ds(start + j, value.shape[0], stride=per), :] = value[
                :, j * LANES : (j + 1) * LANES
            ]

    for c in range(FF // D):
        cols = slice(c * D, (c + 1) * D)
        acc[...] = dot_nn(second[...], wu[:, cols])
        acc2[...] = dot_nt(glow[...], wd[cols, :])
        bias = b_up[:, cols]

        def activate(at, carry, cols=cols, bias=bias):
            pre = acc[at, :] + bias
            cdf = 0.5 * (1.0 + lax.erf(pre * SQRT_HALF))
            hidden[at, cols] = (pre * cdf).astype(BF)
            slope = cdf + pre * INV_ROOT_TAU * jnp.exp(-0.5 * pre * pre)
            back = (acc2[at, :] * slope).astype(BF)
            gpre[at, cols] = back
            return carry + fold_rows(back.astype(F32))

        sums = blocks(activate, jnp.zeros((8, D), F32))
        put_row_vector(wide, R_BU + 3 * c, jnp.sum(sums, axis=0, keepdims=True))
        scatter(dot_tn(second[...], gpre[:, cols]), R_UP + 3 * c, FF // LANES)
        scatter(dot_tn(hidden[:, cols], glow[...]), R_DOWN + 3 * D * c, D // LANES)

    acc[...] = dot_nn(hidden[...], wd[...])
    acc2[...] = dot_nt(gpre[...], wu[...])

    def second_back(at, carry):
        sum_g, sum_b, sum_low, sum_attn = carry
        grad = acc2[at, :]
        hat = n2_s[at, :]
        low = glow[at, :].astype(F32)
        mixed_block = mid_s[at, :] + (acc[at, :] + b_down)
        gmix[at, :] = mixed_block.astype(BF)
        s = grad * g_second
        middle_grad = low + r2_s[at, :] * (
            s
            - jnp.mean(s, axis=-1, keepdims=True)
            - hat * jnp.mean(s * hat, axis=-1, keepdims=True)
        )
        mid_s[at, :] = middle_grad
        attn = middle_grad.astype(BF)
        gattn[at, :] = attn
        return (
            sum_g + fold_rows(grad * hat),
            sum_b + fold_rows(grad),
            sum_low + fold_rows(low),
            sum_attn + fold_rows(attn.astype(F32)),
        )

    zero8 = jnp.zeros((8, D), F32)
    sum_g, sum_b, sum_low, sum_attn = blocks(second_back, (zero8, zero8, zero8, zero8))

    def put_sum(row, value):
        put_row_vector(wide, row, jnp.sum(value, axis=0, keepdims=True))

    put_sum(R_G2, sum_g)
    put_sum(R_B2, sum_b)
    put_sum(R_BD, sum_low)
    put_sum(R_BO, sum_attn)
    for b in range(images):
        out_ref[b] = gmix[b * pad : b * pad + tok, :]

    scatter(dot_tn(mixed[...], gattn[...]), R_OUT, D // LANES)
    gmix[...] = dot_nt(gattn[...], wo[...]).astype(BF)

    for b in range(images):
        for h in range(HEADS // 2):
            query = slab(qkv, b, h * LANES)
            keys = slab(qkv, b, D + h * LANES)
            values = slab(qkv, b, 2 * D + h * LANES)
            grads = slab(gmix, b, h * LANES)
            parts = []
            for s in range(2):
                prob = probs[(b * HEADS // 2 + h) * 2 + s]
                grad_prob = dot_nt(grads * halves[s], values)
                total_s = jnp.sum(grad_prob * prob, axis=-1, keepdims=True)
                grad_score = (prob * (grad_prob - total_s)).astype(BF)
                parts.append(
                    (
                        dot_nn(grad_score, keys) * scale,
                        dot_tn(grad_score, query) * scale,
                        dot_tn(prob.astype(BF), grads),
                    )
                )
            for t in range(3):
                column = t * D + h * LANES
                gj[b * pad : (b + 1) * pad, column : column + LANES] = jnp.where(
                    low_lane, parts[0][t], parts[1][t]
                ).astype(BF)

    for t in range(3):
        scatter(dot_tn(normed[...], gj[:, t * D : (t + 1) * D]), R_QKV + 3 * t, 3 * D // LANES)
    acc[...] = dot_nt(gj[...], wq[...])

    def first_back(at, carry):
        sum_g, sum_b, sum_q, sum_v = carry
        grad = acc[at, :]
        hat = n1_s[at, :]
        s = grad * g_first
        result = mid_s[at, :] + r1_s[at, :] * (
            s
            - jnp.mean(s, axis=-1, keepdims=True)
            - hat * jnp.mean(s * hat, axis=-1, keepdims=True)
        )
        gmix[at, :] = result.astype(BF)
        return (
            sum_g + fold_rows(grad * hat),
            sum_b + fold_rows(grad),
            sum_q + fold_rows(gj[at, :D].astype(F32)),
            sum_v + fold_rows(gj[at, 2 * D :].astype(F32)),
        )

    sum_g, sum_b, sum_q, sum_v = blocks(first_back, (zero8, zero8, zero8, zero8))
    put_sum(R_G1, sum_g)
    put_sum(R_B1, sum_b)
    put_sum(R_BQ, sum_q)
    put_sum(R_BV, sum_v)
    for b in range(images):
        gin_ref[b] = gmix[b * pad : b * pad + tok, :]

    for d in range(devices):
        stage[d] = wide[d * rows : (d + 1) * rows, :].astype(BF)
    copies = [
        pltpu.make_async_copy(stage.at[owner], ref, sems.at[k])
        for k, (ref, owner) in enumerate(slots(shares))
    ]
    for c in copies:
        c.start()
    for c in copies:
        c.wait()


def run_layer(me, counts, images, cotangent, groups, devices, interpret=False):
    rows = groups[0].shape[1]
    count, tok, _ = images.shape
    pad = (tok + 15) // 16 * 16
    total = count * pad
    body = lambda *refs: layer_body(
        *refs, devices=devices, rows=rows, images=count, tok=tok, pad=pad
    )
    vmem = pl.BlockSpec(memory_space=pltpu.VMEM)
    smem = pl.BlockSpec(memory_space=pltpu.SMEM)
    anyspace = pl.BlockSpec(memory_space=pl.ANY)
    parts = tuple(jax.ShapeDtypeStruct(g.shape, BF) for g in groups)
    act = jax.ShapeDtypeStruct(images.shape, BF)
    V = pltpu.VMEM
    scratch = [
        V((devices, rows, LANES), BF),
        V((devices * rows, LANES), F32),
        V((D, 3 * D), BF),
        V((D, D), BF),
        V((D, FF), BF),
        V((FF, D), BF),
        V((total, D), F32),
        V((total, D), F32),
        V((total, 1), F32),
        V((total, D), BF),
        V((total, 3 * D), BF),
        V((count * HEADS, pad, pad), F32),
        V((total, D), BF),
        V((total, D), F32),
        V((total, D), F32),
        V((total, 1), F32),
        V((total, D), BF),
        V((total, FF), BF),
        V((total, FF), BF),
        V((total, D), F32),
        V((total, D), F32),
        V((total, D), BF),
        V((total, D), BF),
        V((total, D), BF),
        V((total, 3 * D), BF),
        pltpu.SemaphoreType.DMA((devices,)),
    ]
    return pl.pallas_call(
        body,
        name="layer",
        out_shape=(act, act) + parts,
        in_specs=[smem, smem, vmem, vmem] + [vmem] * len(groups),
        out_specs=(vmem, vmem) + (anyspace,) * len(groups),
        scratch_shapes=scratch,
        compiler_params=pltpu.CompilerParams(vmem_limit_bytes=48 << 20),
        interpret=interpret,
    )(me, counts, images, cotangent, *groups)


def permute(value, devices, partner):
    return lax.ppermute(value, "dp", [(i, partner(i)) for i in range(devices)])


def over_planes(value, devices, shift):
    return permute(value, devices, lambda i: i ^ (8 * shift))


def over_core(value, devices):
    return permute(value, devices, lambda i: i ^ 1)


def over_first(value, devices):
    return permute(value, devices, lambda i: i ^ (4 if i & 1 else 2))


def over_second(value, devices):
    return permute(value, devices, lambda i: i ^ (2 if i & 1 else 4))


def fence(*values):
    return lax.optimization_barrier(values)


def gather_groups(own, n):
    outer = n // 8
    half = outer // 2
    got = {0: own, half: over_planes(own, n, half)}
    if half > 1:
        got[half // 2] = over_planes(own, n, half // 2)
        names = sorted(got)
        got = dict(zip(names, fence(*[got[s] for s in names])))
    bit = half // 2
    while bit:
        for s in sorted(got):
            if s ^ bit not in got:
                got[s ^ bit] = over_planes(got[s], n, bit)
        bit //= 2
    got = [got[s] for s in range(outer)]
    a = jnp.stack(got[: outer // 2])
    a1 = over_first(a, n)
    an = jnp.concatenate([a, a1], axis=0)
    af = over_second(an, n)
    *rest, an = fence(*got[outer // 2 :], an)
    b = jnp.stack(rest)
    b1 = over_first(b, n)
    bn = jnp.concatenate([b, b1], axis=0)
    bf = over_second(bn, n)
    return [an, af, over_core(an, n), over_core(af, n), bn, bf, over_core(bn, n), over_core(bf, n)]


def reduce_groups(parts, n):
    near, far = parts[:4], parts[4:]

    def add(held, got):
        return held.astype(F32) + got.astype(F32)

    fc = [over_core(far[2], n), over_core(far[3], n)]
    nc = [over_core(near[2], n), over_core(near[3], n)]

    def second_step(keep, got):
        return add(keep[0], got[0]), over_second(add(keep[1], got[1]).astype(BF), n)

    def first_step(held, got):
        total = add(held, got)
        cut = total.shape[0] // 2
        return total[:cut], over_first(total[cut:].astype(BF), n)

    outer = n // 8
    f1 = second_step(far, fc)
    n1 = second_step(near, nc)
    f2 = first_step(*f1)
    n2 = first_step(*n1)
    f3 = add(*f2)
    far = [f3[s] for s in range(outer - outer // 2)]
    bit = outer // 4
    while bit:
        far = [far[s] + over_planes(far[s + bit].astype(BF), n, bit).astype(F32) for s in range(bit)]
        bit //= 2
    last = over_planes(far[0].astype(BF), n, outer // 2)
    n3 = add(*n2)
    near = [n3[s] for s in range(outer // 2)]
    bit = outer // 4
    while bit:
        near = [
            near[s] + over_planes(near[s + bit].astype(BF), n, bit).astype(F32) for s in range(bit)
        ]
        bit //= 2
    total = near[0] + last.astype(F32)
    return total


def on_device(images, params, cotangent, counts):
    devices = lax.axis_size("dp")
    own = params.reshape(-1, LANES)
    groups = gather_groups(own, devices)
    me = lax.axis_index("dp").astype(jnp.int32).reshape(1)
    result, image_grad, *parts = run_layer(me, counts, images, cotangent, groups, devices)
    owned = reduce_groups(parts, devices)
    return (result, image_grad, owned.reshape(-1))


def solution(mesh):
    placed = (P("dp", None, None), P("dp"), P("dp", None, None), P("dp"))
    return jax.shard_map(
        on_device,
        mesh=mesh,
        in_specs=placed,
        out_specs=(P("dp", None, None), P("dp", None, None), P("dp")),
        check_vma=False,
    )
```

```python
import jax
import jax.numpy as jnp
from jax import lax
from jax.experimental import pallas as pl
from jax.experimental.pallas import tpu as pltpu
from jax.sharding import PartitionSpec as P

D = 384
HEADS = 6
FF = 1536
LANES = 128
EPSILON = 1e-06
SQRT_HALF = 0.7071067811865476
INV_ROOT_TAU = 0.3989422804014327
BF = jnp.bfloat16
F32 = jnp.float32

R_QKV = 0
R_BQ = R_QKV + D * 3 * D // LANES
R_BV = R_BQ + D // LANES
R_OUT = R_BV + D // LANES
R_BO = R_OUT + D * D // LANES
R_UP = R_BO + D // LANES
R_BU = R_UP + D * FF // LANES
R_DOWN = R_BU + FF // LANES
R_BD = R_DOWN + D * FF // LANES
R_G1 = R_BD + D // LANES
R_B1 = R_G1 + D // LANES
R_G2 = R_B1 + D // LANES
R_B2 = R_G2 + D // LANES
R_END = R_B2 + D // LANES


def dot_nn(a, b):
    return lax.dot_general(a, b, (((1,), (0,)), ((), ())), preferred_element_type=F32)


def dot_nt(a, b):
    return lax.dot_general(a, b, (((1,), (1,)), ((), ())), preferred_element_type=F32)


def dot_tn(a, b):
    return lax.dot_general(a, b, (((0,), (0,)), ((), ())), preferred_element_type=F32)


def row_vector(ref, row, count):
    return jnp.concatenate([ref[row + i : row + i + 1, :] for i in range(count)], axis=1)


def put_row_vector(ref, row, value):
    for i in range(value.shape[1] // LANES):
        ref[row + i : row + i + 1, :] = value[:, i * LANES : (i + 1) * LANES]


def fold_rows(value):
    return jnp.sum(value.reshape(-1, 8, value.shape[-1]), axis=0)


def low_bits(me, c, b2, b1):
    first = 2 + 2 * ((me & 1) ^ c)
    return (me & 7) ^ c ^ (b1 * first) ^ (b2 * (6 - first))


def group_keys(devices):
    outer = devices // 8
    near, far = tuple(range(outer // 2)), tuple(range(outer // 2, outer))
    return [(c, b2, shifts) for shifts in (near, far) for c in range(2) for b2 in range(2)]


def layer_body(
    me_ref,
    count_ref,
    image_ref,
    cot_ref,
    *refs,
    devices,
    rows,
    images,
    tok,
    pad,
):
    order = group_keys(devices)
    groups = refs[: len(order)]
    refs = refs[len(order) :]
    out_ref, gin_ref = refs[:2]
    shares = refs[2 : 2 + len(order)]
    (
        wide,
        wq,
        wo,
        wu,
        wd,
        x_s,
        n1_s,
        r1_s,
        normed,
        qkv,
        probs,
        mixed,
        mid_s,
        n2_s,
        r2_s,
        second,
        hidden,
        gpre,
        acc,
        acc2,
        glow,
        gattn,
        gmix,
        gj,
    ) = refs[2 + len(order) :]
    me = me_ref[0]
    total = images * pad
    scale = float(D // HEADS) ** (-0.5)
    blk = 32
    steps = total // blk
    plane = me >> 3

    def slots(refs):
        for ref, (c, b2, shifts) in zip(refs, order):
            for i in range(2 * len(shifts)):
                b1, s = divmod(i, len(shifts))
                yield ref.at[i], ((plane ^ shifts[s]) << 3) | low_bits(me, c, b2, b1)

    for b in range(images):
        live = (count_ref[0] > b).astype(F32)
        zeros = jnp.zeros((pad - tok, D), F32)
        x_s[b * pad : (b + 1) * pad, :] = jnp.concatenate(
            [image_ref[b].astype(F32), zeros], axis=0
        )
        glow[b * pad : (b + 1) * pad, :] = jnp.concatenate(
            [cot_ref[b].astype(F32) * live, zeros], axis=0
        ).astype(BF)

    for ref, owner in slots(groups):
        wide[pl.ds(owner * rows, rows), :] = ref[...].astype(F32)

    def unpack(dst, start, height, width):
        per = width // LANES
        for j in range(per):
            dst[:, j * LANES : (j + 1) * LANES] = wide[
                pl.ds(start + j, height, stride=per), :
            ].astype(BF)

    unpack(wq, R_QKV, D, 3 * D)
    unpack(wo, R_OUT, D, D)
    unpack(wu, R_UP, D, FF)
    unpack(wd, R_DOWN, FF, D)
    b_query = row_vector(wide, R_BQ, 3)
    b_value = row_vector(wide, R_BV, 3)
    b_out = row_vector(wide, R_BO, 3)
    b_up = row_vector(wide, R_BU, 12)
    b_down = row_vector(wide, R_BD, 3)
    g_first = row_vector(wide, R_G1, 3)
    b_first = row_vector(wide, R_B1, 3)
    g_second = row_vector(wide, R_G2, 3)
    b_second = row_vector(wide, R_B2, 3)

    def blocks(body, init=None):
        def step(i, carry):
            return body(pl.ds(pl.multiple_of(i * blk, blk), blk), carry)

        return lax.fori_loop(0, steps, step, init, unroll=True)

    def standardize(v):
        centre = v - jnp.mean(v, axis=-1, keepdims=True)
        inverse = lax.rsqrt(jnp.mean(centre * centre, axis=-1, keepdims=True) + EPSILON)
        return centre * inverse, inverse

    def first_norm(at, carry):
        hat, inverse = standardize(x_s[at, :])
        n1_s[at, :] = hat
        r1_s[at, :] = inverse
        normed[at, :] = (hat * g_first + b_first).astype(BF)
        return carry

    blocks(first_norm)

    qkv[:, :D] = (dot_nn(normed[...], wq[:, :D]) + b_query).astype(BF)
    qkv[:, D : 2 * D] = dot_nn(normed[...], wq[:, D : 2 * D]).astype(BF)
    qkv[:, 2 * D :] = (dot_nn(normed[...], wq[:, 2 * D :]) + b_value).astype(BF)

    lane = lax.broadcasted_iota(jnp.int32, (1, LANES), 1)
    low_lane = lane < D // HEADS
    halves = (low_lane.astype(F32).astype(BF), (1.0 - low_lane.astype(F32)).astype(BF))
    key_ok = lax.broadcasted_iota(jnp.int32, (1, pad), 1) < tok

    def slab(ref, b, column):
        return ref[b * pad : (b + 1) * pad, column : column + LANES]

    for b in range(images):
        for h in range(HEADS // 2):
            query = slab(qkv, b, h * LANES)
            keys = slab(qkv, b, D + h * LANES)
            values = slab(qkv, b, 2 * D + h * LANES)
            outs = []
            for s in range(2):
                scores = jnp.where(key_ok, dot_nt(query * halves[s], keys) * scale, -1e30)
                top = jnp.max(scores, axis=-1, keepdims=True)
                weight = jnp.exp(scores - top)
                prob = weight * (1.0 / jnp.sum(weight, axis=-1, keepdims=True))
                probs[(b * HEADS // 2 + h) * 2 + s] = prob
                outs.append(dot_nn(prob.astype(BF), values))
            mixed[b * pad : (b + 1) * pad, h * LANES : (h + 1) * LANES] = jnp.where(
                low_lane, outs[0], outs[1]
            ).astype(BF)

    acc[...] = dot_nn(mixed[...], wo[...])

    def second_norm(at, carry):
        middle = x_s[at, :] + (acc[at, :] + b_out)
        mid_s[at, :] = middle
        hat, inverse = standardize(middle)
        n2_s[at, :] = hat
        r2_s[at, :] = inverse
        second[at, :] = (hat * g_second + b_second).astype(BF)
        return carry

    blocks(second_norm)

    wide[R_END:, :] = jnp.zeros((devices * rows - R_END, LANES), F32)

    def scatter(value, start, per):
        for j in range(value.shape[1] // LANES):
            wide[pl.ds(start + j, value.shape[0], stride=per), :] = value[
                :, j * LANES : (j + 1) * LANES
            ]

    for c in range(FF // D):
        cols = slice(c * D, (c + 1) * D)
        acc[...] = dot_nn(second[...], wu[:, cols])
        acc2[...] = dot_nt(glow[...], wd[cols, :])
        bias = b_up[:, cols]

        def activate(at, carry, cols=cols, bias=bias):
            pre = acc[at, :] + bias
            cdf = 0.5 * (1.0 + lax.erf(pre * SQRT_HALF))
            hidden[at, cols] = (pre * cdf).astype(BF)
            slope = cdf + pre * INV_ROOT_TAU * jnp.exp(-0.5 * pre * pre)
            back = (acc2[at, :] * slope).astype(BF)
            gpre[at, cols] = back
            return carry + fold_rows(back.astype(F32))

        sums = blocks(activate, jnp.zeros((8, D), F32))
        put_row_vector(wide, R_BU + 3 * c, jnp.sum(sums, axis=0, keepdims=True))
        scatter(dot_tn(second[...], gpre[:, cols]), R_UP + 3 * c, FF // LANES)
        scatter(dot_tn(hidden[:, cols], glow[...]), R_DOWN + 3 * D * c, D // LANES)

    acc[...] = dot_nn(hidden[...], wd[...])
    acc2[...] = dot_nt(gpre[...], wu[...])

    def second_back(at, carry):
        sum_g, sum_b, sum_low, sum_attn = carry
        grad = acc2[at, :]
        hat = n2_s[at, :]
        low = glow[at, :].astype(F32)
        mixed_block = mid_s[at, :] + (acc[at, :] + b_down)
        gmix[at, :] = mixed_block.astype(BF)
        s = grad * g_second
        middle_grad = low + r2_s[at, :] * (
            s
            - jnp.mean(s, axis=-1, keepdims=True)
            - hat * jnp.mean(s * hat, axis=-1, keepdims=True)
        )
        mid_s[at, :] = middle_grad
        attn = middle_grad.astype(BF)
        gattn[at, :] = attn
        return (
            sum_g + fold_rows(grad * hat),
            sum_b + fold_rows(grad),
            sum_low + fold_rows(low),
            sum_attn + fold_rows(attn.astype(F32)),
        )

    zero8 = jnp.zeros((8, D), F32)
    sum_g, sum_b, sum_low, sum_attn = blocks(second_back, (zero8, zero8, zero8, zero8))

    def put_sum(row, value):
        put_row_vector(wide, row, jnp.sum(value, axis=0, keepdims=True))

    put_sum(R_G2, sum_g)
    put_sum(R_B2, sum_b)
    put_sum(R_BD, sum_low)
    put_sum(R_BO, sum_attn)
    for b in range(images):
        out_ref[b] = gmix[b * pad : b * pad + tok, :]

    scatter(dot_tn(mixed[...], gattn[...]), R_OUT, D // LANES)
    gmix[...] = dot_nt(gattn[...], wo[...]).astype(BF)

    for b in range(images):
        for h in range(HEADS // 2):
            query = slab(qkv, b, h * LANES)
            keys = slab(qkv, b, D + h * LANES)
            values = slab(qkv, b, 2 * D + h * LANES)
            grads = slab(gmix, b, h * LANES)
            parts = []
            for s in range(2):
                prob = probs[(b * HEADS // 2 + h) * 2 + s]
                grad_prob = dot_nt(grads * halves[s], values)
                total_s = jnp.sum(grad_prob * prob, axis=-1, keepdims=True)
                grad_score = (prob * (grad_prob - total_s)).astype(BF)
                parts.append(
                    (
                        dot_nn(grad_score, keys) * scale,
                        dot_tn(grad_score, query) * scale,
                        dot_tn(prob.astype(BF), grads),
                    )
                )
            for t in range(3):
                column = t * D + h * LANES
                gj[b * pad : (b + 1) * pad, column : column + LANES] = jnp.where(
                    low_lane, parts[0][t], parts[1][t]
                ).astype(BF)

    for t in range(3):
        scatter(dot_tn(normed[...], gj[:, t * D : (t + 1) * D]), R_QKV + 3 * t, 3 * D // LANES)
    acc[...] = dot_nt(gj[...], wq[...])

    def first_back(at, carry):
        sum_g, sum_b, sum_q, sum_v = carry
        grad = acc[at, :]
        hat = n1_s[at, :]
        s = grad * g_first
        result = mid_s[at, :] + r1_s[at, :] * (
            s
            - jnp.mean(s, axis=-1, keepdims=True)
            - hat * jnp.mean(s * hat, axis=-1, keepdims=True)
        )
        gmix[at, :] = result.astype(BF)
        return (
            sum_g + fold_rows(grad * hat),
            sum_b + fold_rows(grad),
            sum_q + fold_rows(gj[at, :D].astype(F32)),
            sum_v + fold_rows(gj[at, 2 * D :].astype(F32)),
        )

    sum_g, sum_b, sum_q, sum_v = blocks(first_back, (zero8, zero8, zero8, zero8))
    put_sum(R_G1, sum_g)
    put_sum(R_B1, sum_b)
    put_sum(R_BQ, sum_q)
    put_sum(R_BV, sum_v)
    for b in range(images):
        gin_ref[b] = gmix[b * pad : b * pad + tok, :]

    for ref, owner in slots(shares):
        ref[...] = wide[pl.ds(owner * rows, rows), :].astype(BF)


def run_layer(me, counts, images, cotangent, groups, devices, interpret=False):
    rows = groups[0].shape[1]
    count, tok, _ = images.shape
    pad = (tok + 15) // 16 * 16
    total = count * pad
    body = lambda *refs: layer_body(
        *refs, devices=devices, rows=rows, images=count, tok=tok, pad=pad
    )
    vmem = pl.BlockSpec(memory_space=pltpu.VMEM)
    smem = pl.BlockSpec(memory_space=pltpu.SMEM)
    parts = tuple(jax.ShapeDtypeStruct(g.shape, BF) for g in groups)
    act = jax.ShapeDtypeStruct(images.shape, BF)
    V = pltpu.VMEM
    scratch = [
        V((devices * rows, LANES), F32),
        V((D, 3 * D), BF),
        V((D, D), BF),
        V((D, FF), BF),
        V((FF, D), BF),
        V((total, D), F32),
        V((total, D), F32),
        V((total, 1), F32),
        V((total, D), BF),
        V((total, 3 * D), BF),
        V((count * HEADS, pad, pad), F32),
        V((total, D), BF),
        V((total, D), F32),
        V((total, D), F32),
        V((total, 1), F32),
        V((total, D), BF),
        V((total, FF), BF),
        V((total, FF), BF),
        V((total, D), F32),
        V((total, D), F32),
        V((total, D), BF),
        V((total, D), BF),
        V((total, D), BF),
        V((total, 3 * D), BF),
    ]
    return pl.pallas_call(
        body,
        name="layer",
        out_shape=(act, act) + parts,
        in_specs=[smem, smem, vmem, vmem] + [vmem] * len(groups),
        out_specs=(vmem, vmem) + (vmem,) * len(groups),
        scratch_shapes=scratch,
        compiler_params=pltpu.CompilerParams(vmem_limit_bytes=32 << 20),
        interpret=interpret,
    )(me, counts, images, cotangent, *groups)


def permute(value, devices, partner):
    return lax.ppermute(value, "dp", [(i, partner(i)) for i in range(devices)])


def over_planes(value, devices, shift):
    return permute(value, devices, lambda i: i ^ (8 * shift))


def over_core(value, devices):
    return permute(value, devices, lambda i: i ^ 1)


def over_first(value, devices):
    return permute(value, devices, lambda i: i ^ (4 if i & 1 else 2))


def over_second(value, devices):
    return permute(value, devices, lambda i: i ^ (2 if i & 1 else 4))


def fence(*values):
    return lax.optimization_barrier(values)


def gather_groups(own, n):
    outer = n // 8
    half = outer // 2
    got = {0: own, half: over_planes(own, n, half)}
    bit = half // 2
    while bit:
        for s in sorted(got):
            if s ^ bit not in got:
                got[s ^ bit] = over_planes(got[s], n, bit)
        bit //= 2
    own_first = over_first(own, n)
    others = jnp.stack([got[s] for s in range(1, half)])
    an = jnp.concatenate([own[None], others, own_first[None], over_first(others, n)], axis=0)
    af = over_second(an, n)
    b = jnp.stack([got[s] for s in range(half, outer)])
    bn = jnp.concatenate([b, over_first(b, n)], axis=0)
    bf = over_second(bn, n)
    return [an, af, over_core(an, n), over_core(af, n), bn, bf, over_core(bn, n), over_core(bf, n)]


def reduce_groups(parts, n):
    near, far = list(parts[:4]), parts[4:]

    def add(held, got):
        return held.astype(F32) + got.astype(F32)

    fc = [over_core(far[2], n), over_core(far[3], n)]
    nc = [over_core(near[2], n), over_core(near[3], n)]

    def second_step(keep, got):
        return add(keep[0], got[0]), over_second(add(keep[1], got[1]).astype(BF), n)

    def first_step(held, got):
        total = add(held, got)
        cut = total.shape[0] // 2
        return total[:cut], over_first(total[cut:].astype(BF), n)

    outer = n // 8
    f1 = second_step(far, fc)
    *f1, near[0], near[1], nc[0], nc[1] = fence(*f1, near[0], near[1], *nc)
    n1 = second_step(near, nc)
    f2 = first_step(*f1)
    n2 = first_step(*n1)
    f3 = add(*f2)
    far = [f3[s] for s in range(outer - outer // 2)]
    bit = outer // 4
    while bit:
        far = [far[s] + over_planes(far[s + bit].astype(BF), n, bit).astype(F32) for s in range(bit)]
        bit //= 2
    last = over_planes(far[0].astype(BF), n, outer // 2)
    n3 = add(*n2)
    near = [n3[s] for s in range(outer // 2)]
    bit = outer // 4
    while bit:
        near = [
            near[s] + over_planes(near[s + bit].astype(BF), n, bit).astype(F32) for s in range(bit)
        ]
        bit //= 2
    total = near[0] + last.astype(F32)
    return total


def on_device(images, params, cotangent, counts):
    devices = lax.axis_size("dp")
    own = params.reshape(-1, LANES)
    groups = gather_groups(own, devices)
    me = lax.axis_index("dp").astype(jnp.int32).reshape(1)
    result, image_grad, *parts = run_layer(me, counts, images, cotangent, groups, devices)
    owned = reduce_groups(parts, devices)
    return (result, image_grad, owned.reshape(-1))


def solution(mesh):
    placed = (P("dp", None, None), P("dp"), P("dp", None, None), P("dp"))
    return jax.shard_map(
        on_device,
        mesh=mesh,
        in_specs=placed,
        out_specs=(P("dp", None, None), P("dp", None, None), P("dp")),
        check_vma=False,
    )
```

```python
import jax
import jax.numpy as jnp
from jax import lax
from jax.experimental import pallas as pl
from jax.experimental.pallas import tpu as pltpu
from jax.sharding import PartitionSpec as P

D = 384
HEADS = 6
FF = 1536
LANES = 128
EPSILON = 1e-06
SQRT_HALF = 0.7071067811865476
INV_ROOT_TAU = 0.3989422804014327
BF = jnp.bfloat16
F32 = jnp.float32

R_QKV = 0
R_BQ = R_QKV + D * 3 * D // LANES
R_BV = R_BQ + D // LANES
R_OUT = R_BV + D // LANES
R_BO = R_OUT + D * D // LANES
R_UP = R_BO + D // LANES
R_BU = R_UP + D * FF // LANES
R_DOWN = R_BU + FF // LANES
R_BD = R_DOWN + D * FF // LANES
R_G1 = R_BD + D // LANES
R_B1 = R_G1 + D // LANES
R_G2 = R_B1 + D // LANES
R_B2 = R_G2 + D // LANES
R_END = R_B2 + D // LANES


def dot_nn(a, b):
    return lax.dot_general(a, b, (((1,), (0,)), ((), ())), preferred_element_type=F32)


def dot_nt(a, b):
    return lax.dot_general(a, b, (((1,), (1,)), ((), ())), preferred_element_type=F32)


def dot_tn(a, b):
    return lax.dot_general(a, b, (((0,), (0,)), ((), ())), preferred_element_type=F32)


def row_vector(ref, row, count):
    return jnp.concatenate([ref[row + i : row + i + 1, :] for i in range(count)], axis=1)


def put_row_vector(ref, row, value):
    for i in range(value.shape[1] // LANES):
        ref[row + i : row + i + 1, :] = value[:, i * LANES : (i + 1) * LANES]


def fold_rows(value):
    return jnp.sum(value.reshape(-1, 8, value.shape[-1]), axis=0)


def low_bits(me, c, b2, b1):
    first = 2 + 2 * ((me & 1) ^ c)
    return (me & 7) ^ c ^ (b1 * first) ^ (b2 * (6 - first))


def group_keys(devices):
    outer = devices // 8
    near, far = tuple(range(outer // 2)), tuple(range(outer // 2, outer))
    return [(c, b2, shifts) for shifts in (near, far) for c in range(2) for b2 in range(2)]


def layer_body(
    me_ref,
    count_ref,
    image_ref,
    cot_ref,
    *refs,
    devices,
    rows,
    images,
    tok,
    pad,
):
    order = group_keys(devices)
    groups = refs[: len(order)]
    refs = refs[len(order) :]
    out_ref, gin_ref = refs[:2]
    shares = refs[2 : 2 + len(order)]
    (
        wide,
        wq,
        wo,
        wu,
        wd,
        x_s,
        n1_s,
        r1_s,
        normed,
        qkv,
        probs,
        mixed,
        mid_s,
        n2_s,
        r2_s,
        second,
        hidden,
        gpre,
        acc,
        acc2,
        glow,
        gattn,
        gmix,
        gj,
    ) = refs[2 + len(order) :]
    me = me_ref[0]
    total = images * pad
    scale = float(D // HEADS) ** (-0.5)
    blk = 32
    steps = total // blk
    plane = me >> 3

    def slots(refs):
        for ref, (c, b2, shifts) in zip(refs, order):
            for i in range(2 * len(shifts)):
                b1, s = divmod(i, len(shifts))
                yield ref.at[i], ((plane ^ shifts[s]) << 3) | low_bits(me, c, b2, b1)

    for b in range(images):
        live = (count_ref[0] > b).astype(F32)
        x_s[b * pad : (b + 1) * pad, :] = image_ref[b].astype(F32)
        glow[b * pad : (b + 1) * pad, :] = (cot_ref[b].astype(F32) * live).astype(BF)

    for ref, owner in slots(groups):
        wide[pl.ds(owner * rows, rows), :] = ref[...].astype(F32)

    def unpack(dst, start, height, width):
        per = width // LANES
        for j in range(per):
            dst[:, j * LANES : (j + 1) * LANES] = wide[
                pl.ds(start + j, height, stride=per), :
            ].astype(BF)

    unpack(wq, R_QKV, D, 3 * D)
    unpack(wo, R_OUT, D, D)
    unpack(wu, R_UP, D, FF)
    unpack(wd, R_DOWN, FF, D)
    b_query = row_vector(wide, R_BQ, 3)
    b_value = row_vector(wide, R_BV, 3)
    b_out = row_vector(wide, R_BO, 3)
    b_up = row_vector(wide, R_BU, 12)
    b_down = row_vector(wide, R_BD, 3)
    g_first = row_vector(wide, R_G1, 3)
    b_first = row_vector(wide, R_B1, 3)
    g_second = row_vector(wide, R_G2, 3)
    b_second = row_vector(wide, R_B2, 3)

    def blocks(body, init=None):
        def step(i, carry):
            return body(pl.ds(pl.multiple_of(i * blk, blk), blk), carry)

        return lax.fori_loop(0, steps, step, init, unroll=True)

    def standardize(v):
        centre = v - jnp.mean(v, axis=-1, keepdims=True)
        inverse = lax.rsqrt(jnp.mean(centre * centre, axis=-1, keepdims=True) + EPSILON)
        return centre * inverse, inverse

    def first_norm(at, carry):
        hat, inverse = standardize(x_s[at, :])
        n1_s[at, :] = hat
        r1_s[at, :] = inverse
        normed[at, :] = (hat * g_first + b_first).astype(BF)
        return carry

    blocks(first_norm)

    qkv[:, :D] = (dot_nn(normed[...], wq[:, :D]) + b_query).astype(BF)
    qkv[:, D : 2 * D] = dot_nn(normed[...], wq[:, D : 2 * D]).astype(BF)
    qkv[:, 2 * D :] = (dot_nn(normed[...], wq[:, 2 * D :]) + b_value).astype(BF)

    lane = lax.broadcasted_iota(jnp.int32, (1, LANES), 1)
    low_lane = lane < D // HEADS
    halves = (low_lane.astype(F32).astype(BF), (1.0 - low_lane.astype(F32)).astype(BF))
    key_ok = lax.broadcasted_iota(jnp.int32, (1, pad), 1) < tok

    def slab(ref, b, column):
        return ref[b * pad : (b + 1) * pad, column : column + LANES]

    for b in range(images):
        for h in range(HEADS // 2):
            query = slab(qkv, b, h * LANES)
            keys = slab(qkv, b, D + h * LANES)
            values = slab(qkv, b, 2 * D + h * LANES)
            both = jnp.concatenate([query * halves[0], query * halves[1]], axis=0)
            scores = jnp.where(key_ok, dot_nt(both, keys) * scale, -1e30)
            top = jnp.max(scores, axis=-1, keepdims=True)
            weight = jnp.exp(scores - top)
            prob = weight * (1.0 / jnp.sum(weight, axis=-1, keepdims=True))
            probs[b * HEADS // 2 + h] = prob
            outs = dot_nn(prob.astype(BF), values)
            mixed[b * pad : (b + 1) * pad, h * LANES : (h + 1) * LANES] = jnp.where(
                low_lane, outs[:pad], outs[pad:]
            ).astype(BF)

    acc[...] = dot_nn(mixed[...], wo[...])

    def second_norm(at, carry):
        middle = x_s[at, :] + (acc[at, :] + b_out)
        mid_s[at, :] = middle
        hat, inverse = standardize(middle)
        n2_s[at, :] = hat
        r2_s[at, :] = inverse
        second[at, :] = (hat * g_second + b_second).astype(BF)
        return carry

    blocks(second_norm)

    wide[R_END:, :] = jnp.zeros((devices * rows - R_END, LANES), F32)

    def scatter(value, start, per):
        for j in range(value.shape[1] // LANES):
            wide[pl.ds(start + j, value.shape[0], stride=per), :] = value[
                :, j * LANES : (j + 1) * LANES
            ]

    for c in range(FF // D):
        cols = slice(c * D, (c + 1) * D)
        acc[...] = dot_nn(second[...], wu[:, cols])
        acc2[...] = dot_nt(glow[...], wd[cols, :])
        bias = b_up[:, cols]

        def activate(at, carry, cols=cols, bias=bias):
            pre = acc[at, :] + bias
            cdf = 0.5 * (1.0 + lax.erf(pre * SQRT_HALF))
            hidden[at, cols] = (pre * cdf).astype(BF)
            slope = cdf + pre * INV_ROOT_TAU * jnp.exp(-0.5 * pre * pre)
            back = (acc2[at, :] * slope).astype(BF)
            gpre[at, cols] = back
            return carry + fold_rows(back.astype(F32))

        sums = blocks(activate, jnp.zeros((8, D), F32))
        put_row_vector(wide, R_BU + 3 * c, jnp.sum(sums, axis=0, keepdims=True))
        scatter(dot_tn(second[...], gpre[:, cols]), R_UP + 3 * c, FF // LANES)
        scatter(dot_tn(hidden[:, cols], glow[...]), R_DOWN + 3 * D * c, D // LANES)

    acc[...] = dot_nn(hidden[...], wd[...])
    acc2[...] = dot_nt(gpre[...], wu[...])

    def second_back(at, carry):
        sum_g, sum_b, sum_low, sum_attn = carry
        grad = acc2[at, :]
        hat = n2_s[at, :]
        low = glow[at, :].astype(F32)
        mixed_block = mid_s[at, :] + (acc[at, :] + b_down)
        gmix[at, :] = mixed_block.astype(BF)
        s = grad * g_second
        middle_grad = low + r2_s[at, :] * (
            s
            - jnp.mean(s, axis=-1, keepdims=True)
            - hat * jnp.mean(s * hat, axis=-1, keepdims=True)
        )
        mid_s[at, :] = middle_grad
        attn = middle_grad.astype(BF)
        gattn[at, :] = attn
        return (
            sum_g + fold_rows(grad * hat),
            sum_b + fold_rows(grad),
            sum_low + fold_rows(low),
            sum_attn + fold_rows(attn.astype(F32)),
        )

    zero8 = jnp.zeros((8, D), F32)
    sum_g, sum_b, sum_low, sum_attn = blocks(second_back, (zero8, zero8, zero8, zero8))

    def put_sum(row, value):
        put_row_vector(wide, row, jnp.sum(value, axis=0, keepdims=True))

    put_sum(R_G2, sum_g)
    put_sum(R_B2, sum_b)
    put_sum(R_BD, sum_low)
    put_sum(R_BO, sum_attn)
    for b in range(images):
        out_ref[b] = gmix[b * pad : b * pad + tok, :]

    scatter(dot_tn(mixed[...], gattn[...]), R_OUT, D // LANES)
    gmix[...] = dot_nt(gattn[...], wo[...]).astype(BF)

    for b in range(images):
        for h in range(HEADS // 2):
            query = slab(qkv, b, h * LANES)
            keys = slab(qkv, b, D + h * LANES)
            values = slab(qkv, b, 2 * D + h * LANES)
            grads = slab(gmix, b, h * LANES)
            both = jnp.concatenate([grads * halves[0], grads * halves[1]], axis=0)
            both_query = jnp.concatenate([query * halves[0], query * halves[1]], axis=0)
            prob = probs[b * HEADS // 2 + h]
            grad_prob = dot_nt(both, values)
            total_s = jnp.sum(grad_prob * prob, axis=-1, keepdims=True)
            grad_score = (prob * (grad_prob - total_s)).astype(BF)
            grad_query = dot_nn(grad_score, keys) * scale
            found = (
                jnp.where(low_lane, grad_query[:pad], grad_query[pad:]),
                dot_tn(grad_score, both_query) * scale,
                dot_tn(prob.astype(BF), both),
            )
            for t in range(3):
                column = t * D + h * LANES
                gj[b * pad : (b + 1) * pad, column : column + LANES] = found[t].astype(BF)

    for t in range(3):
        scatter(dot_tn(normed[...], gj[:, t * D : (t + 1) * D]), R_QKV + 3 * t, 3 * D // LANES)
    acc[...] = dot_nt(gj[...], wq[...])

    def first_back(at, carry):
        sum_g, sum_b, sum_q, sum_v = carry
        grad = acc[at, :]
        hat = n1_s[at, :]
        s = grad * g_first
        result = mid_s[at, :] + r1_s[at, :] * (
            s
            - jnp.mean(s, axis=-1, keepdims=True)
            - hat * jnp.mean(s * hat, axis=-1, keepdims=True)
        )
        gmix[at, :] = result.astype(BF)
        return (
            sum_g + fold_rows(grad * hat),
            sum_b + fold_rows(grad),
            sum_q + fold_rows(gj[at, :D].astype(F32)),
            sum_v + fold_rows(gj[at, 2 * D :].astype(F32)),
        )

    sum_g, sum_b, sum_q, sum_v = blocks(first_back, (zero8, zero8, zero8, zero8))
    put_sum(R_G1, sum_g)
    put_sum(R_B1, sum_b)
    put_sum(R_BQ, sum_q)
    put_sum(R_BV, sum_v)
    for b in range(images):
        gin_ref[b] = gmix[b * pad : b * pad + tok, :]

    for ref, owner in slots(shares):
        ref[...] = wide[pl.ds(owner * rows, rows), :].astype(BF)


def run_layer(me, counts, images, cotangent, tok, groups, devices, interpret=False):
    rows = groups[0].shape[1]
    count, pad, _ = images.shape
    total = count * pad
    body = lambda *refs: layer_body(
        *refs, devices=devices, rows=rows, images=count, tok=tok, pad=pad
    )
    vmem = pl.BlockSpec(memory_space=pltpu.VMEM)
    smem = pl.BlockSpec(memory_space=pltpu.SMEM)
    parts = tuple(jax.ShapeDtypeStruct(g.shape, BF) for g in groups)
    act = jax.ShapeDtypeStruct((count, tok, D), BF)
    V = pltpu.VMEM
    scratch = [
        V((devices * rows, LANES), F32),
        V((D, 3 * D), BF),
        V((D, D), BF),
        V((D, FF), BF),
        V((FF, D), BF),
        V((total, D), F32),
        V((total, D), F32),
        V((total, 1), F32),
        V((total, D), BF),
        V((total, 3 * D), BF),
        V((count * HEADS // 2, 2 * pad, pad), F32),
        V((total, D), BF),
        V((total, D), F32),
        V((total, D), F32),
        V((total, 1), F32),
        V((total, D), BF),
        V((total, FF), BF),
        V((total, FF), BF),
        V((total, D), F32),
        V((total, D), F32),
        V((total, D), BF),
        V((total, D), BF),
        V((total, D), BF),
        V((total, 3 * D), BF),
    ]
    return pl.pallas_call(
        body,
        name="layer",
        out_shape=(act, act) + parts,
        in_specs=[smem, smem, vmem, vmem] + [vmem] * len(groups),
        out_specs=(vmem, vmem) + (vmem,) * len(groups),
        scratch_shapes=scratch,
        compiler_params=pltpu.CompilerParams(vmem_limit_bytes=32 << 20),
        interpret=interpret,
    )(me, counts, images, cotangent, *groups)


def permute(value, devices, partner):
    return lax.ppermute(value, "dp", [(i, partner(i)) for i in range(devices)])


def over_planes(value, devices, shift):
    return permute(value, devices, lambda i: i ^ (8 * shift))


def over_core(value, devices):
    return permute(value, devices, lambda i: i ^ 1)


def over_first(value, devices):
    return permute(value, devices, lambda i: i ^ (4 if i & 1 else 2))


def over_second(value, devices):
    return permute(value, devices, lambda i: i ^ (2 if i & 1 else 4))


def fence(*values):
    return lax.optimization_barrier(values)


def gather_groups(own, n, *ready):
    outer = n // 8
    half = outer // 2
    got = {0: own, half: over_planes(own, n, half)}
    bit = half // 2
    while bit:
        for s in sorted(got):
            if s ^ bit not in got:
                got[s ^ bit] = over_planes(got[s], n, bit)
        bit //= 2
    own_first = over_first(own, n)
    others = jnp.stack([got[s] for s in range(1, half)])
    an = jnp.concatenate([own[None], others, own_first[None], over_first(others, n)], axis=0)
    af = over_second(an, n)
    b = jnp.stack([got[s] for s in range(half, outer)])
    bn = jnp.concatenate([b, over_first(b, n)], axis=0)
    bn, *ready = fence(bn, *ready)
    bf = over_second(bn, n)
    groups = [an, af, over_core(an, n), over_core(af, n)]
    groups += [bn, bf, over_core(bn, n), over_core(bf, n)]
    return groups, *ready


def reduce_groups(parts, n):
    near, far = list(parts[:4]), parts[4:]

    def add(held, got):
        return held.astype(F32) + got.astype(F32)

    fc = [over_core(far[2], n), over_core(far[3], n)]
    nc = [over_core(near[2], n), over_core(near[3], n)]

    def second_step(keep, got):
        return add(keep[0], got[0]), over_second(add(keep[1], got[1]).astype(BF), n)

    def first_step(held, got):
        total = add(held, got)
        cut = total.shape[0] // 2
        return total[:cut], over_first(total[cut:].astype(BF), n)

    outer = n // 8
    f1 = second_step(far, fc)
    n1 = second_step(near, nc)
    f2 = first_step(*f1)
    n1 = list(n1)
    *f2, n1[1] = fence(*f2, n1[1])
    n2 = first_step(*n1)
    f3 = add(*f2)
    far = [f3[s] for s in range(outer - outer // 2)]
    bit = outer // 4
    while bit:
        far = [far[s] + over_planes(far[s + bit].astype(BF), n, bit).astype(F32) for s in range(bit)]
        bit //= 2
    last = over_planes(far[0].astype(BF), n, outer // 2)
    n3 = add(*n2)
    near = [n3[s] for s in range(outer // 2)]
    bit = outer // 4
    while bit:
        near = [
            near[s] + over_planes(near[s + bit].astype(BF), n, bit).astype(F32) for s in range(bit)
        ]
        bit //= 2
    total = near[0] + last.astype(F32)
    return total


def on_device(images, params, cotangent, counts):
    devices = lax.axis_size("dp")
    own = params.reshape(-1, LANES)
    tok = images.shape[1]
    blank = ((0, 0), (0, (tok + 15) // 16 * 16 - tok), (0, 0))
    groups, images, cotangent = gather_groups(
        own, devices, jnp.pad(images, blank), jnp.pad(cotangent, blank)
    )
    me = lax.axis_index("dp").astype(jnp.int32).reshape(1)
    result, image_grad, *parts = run_layer(me, counts, images, cotangent, tok, groups, devices)
    owned = reduce_groups(parts, devices)
    return (result, image_grad, owned.reshape(-1))


def solution(mesh):
    placed = (P("dp", None, None), P("dp"), P("dp", None, None), P("dp"))
    return jax.shard_map(
        on_device,
        mesh=mesh,
        in_specs=placed,
        out_specs=(P("dp", None, None), P("dp", None, None), P("dp")),
        check_vma=False,
    )
```

```python
import jax
import jax.numpy as jnp
from jax import lax
from jax.experimental import pallas as pl
from jax.experimental.pallas import tpu as pltpu
from jax.sharding import PartitionSpec as P

D = 384
HEADS = 6
FF = 1536
LANES = 128
EPSILON = 1e-06
SQRT_HALF = 0.7071067811865476
INV_ROOT_TAU = 0.3989422804014327
BF = jnp.bfloat16
F32 = jnp.float32

R_QKV = 0
R_BQ = R_QKV + D * 3 * D // LANES
R_BV = R_BQ + D // LANES
R_OUT = R_BV + D // LANES
R_BO = R_OUT + D * D // LANES
R_UP = R_BO + D // LANES
R_BU = R_UP + D * FF // LANES
R_DOWN = R_BU + FF // LANES
R_BD = R_DOWN + D * FF // LANES
R_G1 = R_BD + D // LANES
R_B1 = R_G1 + D // LANES
R_G2 = R_B1 + D // LANES
R_B2 = R_G2 + D // LANES
R_END = R_B2 + D // LANES


def dot_nn(a, b):
    return lax.dot_general(a, b, (((1,), (0,)), ((), ())), preferred_element_type=F32)


def dot_nt(a, b):
    return lax.dot_general(a, b, (((1,), (1,)), ((), ())), preferred_element_type=F32)


def dot_tn(a, b):
    return lax.dot_general(a, b, (((0,), (0,)), ((), ())), preferred_element_type=F32)


def row_vector(ref, row, count):
    return jnp.concatenate([ref[row + i : row + i + 1, :] for i in range(count)], axis=1)


def put_row_vector(ref, row, value):
    for i in range(value.shape[1] // LANES):
        ref[row + i : row + i + 1, :] = value[:, i * LANES : (i + 1) * LANES]


def fold_rows(value):
    return jnp.sum(value.reshape(-1, 8, value.shape[-1]), axis=0)


def low_bits(me, c, b2, b1):
    first = 2 + 2 * ((me & 1) ^ c)
    return (me & 7) ^ c ^ (b1 * first) ^ (b2 * (6 - first))


def group_keys(devices):
    outer = devices // 8
    near, far = tuple(range(outer // 2)), tuple(range(outer // 2, outer))
    return [(c, b2, shifts) for shifts in (near, far) for c in range(2) for b2 in range(2)]


def layer_body(
    me_ref,
    count_ref,
    image_ref,
    cot_ref,
    *refs,
    devices,
    rows,
    images,
    tok,
    pad,
):
    order = group_keys(devices)
    groups = refs[: len(order)]
    refs = refs[len(order) :]
    out_ref, gin_ref = refs[:2]
    shares = refs[2 : 2 + len(order)]
    (
        wide,
        wq,
        wo,
        wu,
        wd,
        x_s,
        n1_s,
        r1_s,
        normed,
        qkv,
        probs,
        mixed,
        mid_s,
        n2_s,
        r2_s,
        second,
        hidden,
        gpre,
        acc,
        acc2,
        glow,
        gattn,
        gmix,
        gj,
    ) = refs[2 + len(order) :]
    me = me_ref[0]
    total = images * pad
    scale = float(D // HEADS) ** (-0.5)
    blk = 16
    steps = total // blk
    plane = me >> 3

    def slots(refs):
        for ref, (c, b2, shifts) in zip(refs, order):
            for i in range(2 * len(shifts)):
                b1, s = divmod(i, len(shifts))
                yield ref.at[i], ((plane ^ shifts[s]) << 3) | low_bits(me, c, b2, b1)

    for b in range(images):
        live = (count_ref[0] > b).astype(F32)
        x_s[b * pad : (b + 1) * pad, :] = image_ref[b].astype(F32)
        glow[b * pad : (b + 1) * pad, :] = (cot_ref[b].astype(F32) * live).astype(BF)

    for ref, owner in slots(groups):
        wide[pl.ds(owner * rows, rows), :] = ref[...].astype(F32)

    def unpack(dst, start, height, width):
        per = width // LANES
        for j in range(per):
            dst[:, j * LANES : (j + 1) * LANES] = wide[
                pl.ds(start + j, height, stride=per), :
            ].astype(BF)

    unpack(wq, R_QKV, D, 3 * D)
    unpack(wo, R_OUT, D, D)
    unpack(wu, R_UP, D, FF)
    unpack(wd, R_DOWN, FF, D)
    b_query = row_vector(wide, R_BQ, 3)
    b_value = row_vector(wide, R_BV, 3)
    b_out = row_vector(wide, R_BO, 3)
    b_up = row_vector(wide, R_BU, 12)
    b_down = row_vector(wide, R_BD, 3)
    g_first = row_vector(wide, R_G1, 3)
    b_first = row_vector(wide, R_B1, 3)
    g_second = row_vector(wide, R_G2, 3)
    b_second = row_vector(wide, R_B2, 3)

    def blocks(body, init=None):
        def step(i, carry):
            return body(pl.ds(pl.multiple_of(i * blk, blk), blk), carry)

        return lax.fori_loop(0, steps, step, init, unroll=True)

    def standardize(v):
        centre = v - jnp.mean(v, axis=-1, keepdims=True)
        inverse = lax.rsqrt(jnp.mean(centre * centre, axis=-1, keepdims=True) + EPSILON)
        return centre * inverse, inverse

    def first_norm(at, carry):
        hat, inverse = standardize(x_s[at, :])
        n1_s[at, :] = hat
        r1_s[at, :] = inverse
        normed[at, :] = (hat * g_first + b_first).astype(BF)
        return carry

    blocks(first_norm)

    qkv[:, :D] = (dot_nn(normed[...], wq[:, :D]) + b_query).astype(BF)
    qkv[:, D : 2 * D] = dot_nn(normed[...], wq[:, D : 2 * D]).astype(BF)
    qkv[:, 2 * D :] = (dot_nn(normed[...], wq[:, 2 * D :]) + b_value).astype(BF)

    lane = lax.broadcasted_iota(jnp.int32, (1, LANES), 1)
    low_lane = lane < D // HEADS
    halves = (low_lane.astype(F32).astype(BF), (1.0 - low_lane.astype(F32)).astype(BF))
    key_ok = lax.broadcasted_iota(jnp.int32, (1, pad), 1) < tok

    def slab(ref, b, column):
        return ref[b * pad : (b + 1) * pad, column : column + LANES]

    for b in range(images):
        for h in range(HEADS // 2):
            query = slab(qkv, b, h * LANES)
            keys = slab(qkv, b, D + h * LANES)
            values = slab(qkv, b, 2 * D + h * LANES)
            both = jnp.concatenate([query * halves[0], query * halves[1]], axis=0)
            scores = jnp.where(key_ok, dot_nt(both, keys) * scale, -1e30)
            top = jnp.max(scores, axis=-1, keepdims=True)
            weight = jnp.exp(scores - top)
            prob = weight * (1.0 / jnp.sum(weight, axis=-1, keepdims=True))
            probs[b * HEADS // 2 + h] = prob
            outs = dot_nn(prob.astype(BF), values)
            mixed[b * pad : (b + 1) * pad, h * LANES : (h + 1) * LANES] = jnp.where(
                low_lane, outs[:pad], outs[pad:]
            ).astype(BF)

    acc[...] = dot_nn(mixed[...], wo[...])

    def second_norm(at, carry):
        middle = x_s[at, :] + (acc[at, :] + b_out)
        mid_s[at, :] = middle
        hat, inverse = standardize(middle)
        n2_s[at, :] = hat
        r2_s[at, :] = inverse
        second[at, :] = (hat * g_second + b_second).astype(BF)
        return carry

    blocks(second_norm)

    wide[R_END:, :] = jnp.zeros((devices * rows - R_END, LANES), F32)

    def scatter(value, start, per):
        for j in range(value.shape[1] // LANES):
            wide[pl.ds(start + j, value.shape[0], stride=per), :] = value[
                :, j * LANES : (j + 1) * LANES
            ]

    for c in range(FF // D):
        cols = slice(c * D, (c + 1) * D)
        acc[...] = dot_nn(second[...], wu[:, cols])
        acc2[...] = dot_nt(glow[...], wd[cols, :])
        bias = b_up[:, cols]

        def activate(at, carry, cols=cols, bias=bias):
            pre = acc[at, :] + bias
            cdf = 0.5 * (1.0 + lax.erf(pre * SQRT_HALF))
            hidden[at, cols] = (pre * cdf).astype(BF)
            slope = cdf + pre * INV_ROOT_TAU * jnp.exp(-0.5 * pre * pre)
            back = (acc2[at, :] * slope).astype(BF)
            gpre[at, cols] = back
            return carry + fold_rows(back.astype(F32))

        sums = blocks(activate, jnp.zeros((8, D), F32))
        put_row_vector(wide, R_BU + 3 * c, jnp.sum(sums, axis=0, keepdims=True))
        scatter(dot_tn(second[...], gpre[:, cols]), R_UP + 3 * c, FF // LANES)
        scatter(dot_tn(hidden[:, cols], glow[...]), R_DOWN + 3 * D * c, D // LANES)

    acc[...] = dot_nn(hidden[...], wd[...])
    acc2[...] = dot_nt(gpre[...], wu[...])

    def second_back(at, carry):
        sum_g, sum_b, sum_low, sum_attn = carry
        grad = acc2[at, :]
        hat = n2_s[at, :]
        low = glow[at, :].astype(F32)
        mixed_block = mid_s[at, :] + (acc[at, :] + b_down)
        gmix[at, :] = mixed_block.astype(BF)
        s = grad * g_second
        middle_grad = low + r2_s[at, :] * (
            s
            - jnp.mean(s, axis=-1, keepdims=True)
            - hat * jnp.mean(s * hat, axis=-1, keepdims=True)
        )
        mid_s[at, :] = middle_grad
        attn = middle_grad.astype(BF)
        gattn[at, :] = attn
        return (
            sum_g + fold_rows(grad * hat),
            sum_b + fold_rows(grad),
            sum_low + fold_rows(low),
            sum_attn + fold_rows(attn.astype(F32)),
        )

    zero8 = jnp.zeros((8, D), F32)
    sum_g, sum_b, sum_low, sum_attn = blocks(second_back, (zero8, zero8, zero8, zero8))

    def put_sum(row, value):
        put_row_vector(wide, row, jnp.sum(value, axis=0, keepdims=True))

    put_sum(R_G2, sum_g)
    put_sum(R_B2, sum_b)
    put_sum(R_BD, sum_low)
    put_sum(R_BO, sum_attn)
    for b in range(images):
        out_ref[b] = gmix[b * pad : b * pad + tok, :]

    scatter(dot_tn(mixed[...], gattn[...]), R_OUT, D // LANES)
    gmix[...] = dot_nt(gattn[...], wo[...]).astype(BF)

    for b in range(images):
        for h in range(HEADS // 2):
            query = slab(qkv, b, h * LANES)
            keys = slab(qkv, b, D + h * LANES)
            values = slab(qkv, b, 2 * D + h * LANES)
            grads = slab(gmix, b, h * LANES)
            both = jnp.concatenate([grads * halves[0], grads * halves[1]], axis=0)
            both_query = jnp.concatenate([query * halves[0], query * halves[1]], axis=0)
            prob = probs[b * HEADS // 2 + h]
            grad_prob = dot_nt(both, values)
            total_s = jnp.sum(grad_prob * prob, axis=-1, keepdims=True)
            grad_score = (prob * (grad_prob - total_s)).astype(BF)
            grad_query = dot_nn(grad_score, keys) * scale
            found = (
                jnp.where(low_lane, grad_query[:pad], grad_query[pad:]),
                dot_tn(grad_score, both_query) * scale,
                dot_tn(prob.astype(BF), both),
            )
            for t in range(3):
                column = t * D + h * LANES
                gj[b * pad : (b + 1) * pad, column : column + LANES] = found[t].astype(BF)

    for t in range(3):
        scatter(dot_tn(normed[...], gj[:, t * D : (t + 1) * D]), R_QKV + 3 * t, 3 * D // LANES)
    acc[...] = dot_nt(gj[...], wq[...])

    def first_back(at, carry):
        sum_g, sum_b, sum_q, sum_v = carry
        grad = acc[at, :]
        hat = n1_s[at, :]
        s = grad * g_first
        result = mid_s[at, :] + r1_s[at, :] * (
            s
            - jnp.mean(s, axis=-1, keepdims=True)
            - hat * jnp.mean(s * hat, axis=-1, keepdims=True)
        )
        gmix[at, :] = result.astype(BF)
        return (
            sum_g + fold_rows(grad * hat),
            sum_b + fold_rows(grad),
            sum_q + fold_rows(gj[at, :D].astype(F32)),
            sum_v + fold_rows(gj[at, 2 * D :].astype(F32)),
        )

    sum_g, sum_b, sum_q, sum_v = blocks(first_back, (zero8, zero8, zero8, zero8))
    put_sum(R_G1, sum_g)
    put_sum(R_B1, sum_b)
    put_sum(R_BQ, sum_q)
    put_sum(R_BV, sum_v)
    for b in range(images):
        gin_ref[b] = gmix[b * pad : b * pad + tok, :]

    for ref, owner in slots(shares):
        ref[...] = wide[pl.ds(owner * rows, rows), :].astype(BF)


def run_layer(me, counts, images, cotangent, tok, groups, devices, interpret=False):
    rows = groups[0].shape[1]
    count, pad, _ = images.shape
    total = count * pad
    body = lambda *refs: layer_body(
        *refs, devices=devices, rows=rows, images=count, tok=tok, pad=pad
    )
    vmem = pl.BlockSpec(memory_space=pltpu.VMEM)
    smem = pl.BlockSpec(memory_space=pltpu.SMEM)
    parts = tuple(jax.ShapeDtypeStruct(g.shape, BF) for g in groups)
    act = jax.ShapeDtypeStruct((count, tok, D), BF)
    V = pltpu.VMEM
    scratch = [
        V((devices * rows, LANES), F32),
        V((D, 3 * D), BF),
        V((D, D), BF),
        V((D, FF), BF),
        V((FF, D), BF),
        V((total, D), F32),
        V((total, D), F32),
        V((total, 1), F32),
        V((total, D), BF),
        V((total, 3 * D), BF),
        V((count * HEADS // 2, 2 * pad, pad), F32),
        V((total, D), BF),
        V((total, D), F32),
        V((total, D), F32),
        V((total, 1), F32),
        V((total, D), BF),
        V((total, FF), BF),
        V((total, FF), BF),
        V((total, D), F32),
        V((total, D), F32),
        V((total, D), BF),
        V((total, D), BF),
        V((total, D), BF),
        V((total, 3 * D), BF),
    ]
    return pl.pallas_call(
        body,
        name="layer",
        out_shape=(act, act) + parts,
        in_specs=[smem, smem, vmem, vmem] + [vmem] * len(groups),
        out_specs=(vmem, vmem) + (vmem,) * len(groups),
        scratch_shapes=scratch,
        compiler_params=pltpu.CompilerParams(vmem_limit_bytes=32 << 20),
        interpret=interpret,
    )(me, counts, images, cotangent, *groups)


def permute(value, devices, partner):
    return lax.ppermute(value, "dp", [(i, partner(i)) for i in range(devices)])


def over_planes(value, devices, shift):
    return permute(value, devices, lambda i: i ^ (8 * shift))


def over_core(value, devices):
    return permute(value, devices, lambda i: i ^ 1)


def over_first(value, devices):
    return permute(value, devices, lambda i: i ^ (4 if i & 1 else 2))


def over_second(value, devices):
    return permute(value, devices, lambda i: i ^ (2 if i & 1 else 4))


def fence(*values):
    return lax.optimization_barrier(values)


def gather_groups(own, n, *ready):
    outer = n // 8
    half = outer // 2
    got = {0: own, half: over_planes(own, n, half)}
    bit = half // 2
    while bit:
        for s in sorted(got):
            if s ^ bit not in got:
                got[s ^ bit] = over_planes(got[s], n, bit)
        bit //= 2
    own_first = over_first(own, n)
    others = jnp.stack([got[s] for s in range(1, half)])
    an = jnp.concatenate([own[None], others, own_first[None], over_first(others, n)], axis=0)
    af = over_second(an, n)
    b = jnp.stack([got[s] for s in range(half, outer)])
    bn = jnp.concatenate([b, over_first(b, n)], axis=0)
    bn, *ready = fence(bn, *ready)
    bf = over_second(bn, n)
    groups = [an, af, over_core(an, n), over_core(af, n)]
    groups += [bn, bf, over_core(bn, n), over_core(bf, n)]
    return groups, *ready


def reduce_groups(parts, n):
    near, far = list(parts[:4]), parts[4:]

    def add(held, got):
        return held.astype(F32) + got.astype(F32)

    fc = [over_core(far[2], n), over_core(far[3], n)]
    nc = [over_core(near[2], n), over_core(near[3], n)]

    def second_step(keep, got):
        return add(keep[0], got[0]), over_second(add(keep[1], got[1]).astype(BF), n)

    def first_step(held, got):
        total = add(held, got)
        cut = total.shape[0] // 2
        return total[:cut], over_first(total[cut:].astype(BF), n)

    outer = n // 8
    f1 = second_step(far, fc)
    n1 = second_step(near, nc)
    f2 = first_step(*f1)
    n1 = list(n1)
    *f2, n1[1] = fence(*f2, n1[1])
    n2 = first_step(*n1)
    f3 = add(*f2)
    far = [f3[s] for s in range(outer - outer // 2)]
    bit = outer // 4
    while bit:
        far = [far[s] + over_planes(far[s + bit].astype(BF), n, bit).astype(F32) for s in range(bit)]
        bit //= 2
    last = over_planes(far[0].astype(BF), n, outer // 2)
    n3 = add(*n2)
    near = [n3[s] for s in range(outer // 2)]
    bit = outer // 4
    while bit:
        near = [
            near[s] + over_planes(near[s + bit].astype(BF), n, bit).astype(F32) for s in range(bit)
        ]
        bit //= 2
    total = near[0] + last.astype(F32)
    return total


def on_device(images, params, cotangent, counts):
    devices = lax.axis_size("dp")
    own = params.reshape(-1, LANES)
    tok = images.shape[1]
    blank = ((0, 0), (0, (tok + 15) // 16 * 16 - tok), (0, 0))
    groups, images, cotangent = gather_groups(
        own, devices, jnp.pad(images, blank), jnp.pad(cotangent, blank)
    )
    me = lax.axis_index("dp").astype(jnp.int32).reshape(1)
    result, image_grad, *parts = run_layer(me, counts, images, cotangent, tok, groups, devices)
    owned = reduce_groups(parts, devices)
    return (result, image_grad, owned.reshape(-1))


def solution(mesh):
    placed = (P("dp", None, None), P("dp"), P("dp", None, None), P("dp"))
    return jax.shard_map(
        on_device,
        mesh=mesh,
        in_specs=placed,
        out_specs=(P("dp", None, None), P("dp", None, None), P("dp")),
        check_vma=False,
    )
```
